32 devices in a mesh: ctx: 8 (over z, core), head: 4 (over y, x).
Axes of the slice: x: 2, y: 2, z: 4, core: 2. Of those that a mesh axis runs over, the one named last changes fastest.
Arguments:
- query_rows: bfloat16 [2048, 8192], P(('ctx', 'head')), may hold values from -120.5 to 120.5
- key_rows: bfloat16 [2048, 8192], P(('ctx', 'head')), may hold values from -4.1 to 4.1
- value_rows: bfloat16 [2048, 8192], P(('ctx', 'head')), may hold values from -5 to 5
- ssd_input: bfloat16 [2048, 8192], P(('ctx', 'head')), may hold values from -5 to 5
- state_write: bfloat16 [2048, 1024], P(('ctx', 'head')), may hold values from -0.5 to 0.5
- state_read: bfloat16 [2048, 1024], P(('ctx', 'head')), may hold values from -0.125 to 0.125
- step_size: bfloat16 [2048, 128], P(('ctx', 'head')), may hold values from 0.25 to 1
- decay_log: bfloat16 [2048, 128], P(('ctx', 'head')), may hold values from -1 to 0, as said below
- skip_gain: float32 [128], P('head'), may hold values from 0.1 to 0.5
Outputs:
- attended: bfloat16 [2048, 8192], P(('ctx', 'head'))
- scanned: bfloat16 [2048, 8192], P(('ctx', 'head'))
The draws below stay inside these ranges and needn't reach their ends.
Inputs may be any that keep to these rules, and one draw needn't show every extreme that they name: `decay_log`: every entry is negative.
All inputs are finite; a program needn't handle non-finite values.
Results may differ from the reference program's by a relative error of at most 0.008.
Values may be sent and summed in bfloat16 or wider, within the bound.
No kernel may reach another device: no remote copies, remote signals or barrier semaphores. Data moves between devices by JAX's collectives and lax.ppermute only.
A program may use at most 128 MiB of HBM per device.

```python
import math
import jax
import jax.numpy as jnp
from jax import lax

TOK_DEV = 64
HA = 64
HD = 128
SPACE_HEADS = 128
SSD_HEAD_DIM = 64
STATE = 128
GROUPS = 8
STRETCH = 256
REACH = 4
BLOCK_LEN = 256
SEQUENCE_TOKENS = 2048


def drawn_parts(key):
    base_keys = jnp.clip(jax.random.normal(jax.random.fold_in(key, 11), (SEQUENCE_TOKENS, HA * HD), jnp.float32), -4.0, 4.0)
    return base_keys


def draw_key_rows(key, part):
    base_keys = drawn_parts(key)
    result = base_keys
    return result.astype(jnp.bfloat16)


def draw_query_rows(key, part):
    drawn = jnp.clip(jax.random.normal(jax.random.fold_in(key, 13), (SEQUENCE_TOKENS, HA * HD), jnp.float32), -4.0, 4.0)
    result = drawn
    return result.astype(jnp.bfloat16)


def draw_decay_log(key, part):
    slow_share = 0.5
    gradual_heads = jax.random.uniform(jax.random.fold_in(key, 21), (1, SPACE_HEADS), jnp.float32) < slow_share
    gradual_decay_rate = jax.random.uniform(jax.random.fold_in(key, 22), (SEQUENCE_TOKENS, SPACE_HEADS), jnp.float32, 0.05, 0.5) / SEQUENCE_TOKENS
    quick_decay_rate = jnp.exp(jax.random.uniform(jax.random.fold_in(key, 23), (SEQUENCE_TOKENS, SPACE_HEADS), jnp.float32, math.log(0.02), math.log(0.06)))
    block_multiplier = jnp.exp(jax.random.uniform(jax.random.fold_in(key, 24), (SEQUENCE_TOKENS // TOK_DEV, 1), jnp.float32, -math.log(2.0), math.log(2.0)))
    block_multiplier = jnp.repeat(block_multiplier, TOK_DEV, axis=0)
    surge_position = jax.random.randint(jax.random.fold_in(key, 25), (3,), 0, SEQUENCE_TOKENS)
    surge_window = jnp.any(jnp.arange(SEQUENCE_TOKENS)[:, None] == surge_position[None, :], axis=1, keepdims=True)
    surge_length = jax.random.uniform(jax.random.fold_in(key, 26), (SEQUENCE_TOKENS, SPACE_HEADS), jnp.float32, 0.22, 0.69)
    decay_rate = jnp.where(gradual_heads, gradual_decay_rate, quick_decay_rate) * block_multiplier + jnp.where(surge_window, surge_length, 0.0)
    return (-decay_rate).astype(jnp.bfloat16)


def levels(key, dims, split, least, top_value):
    gain = 1.0
    for position, shards_of in split:
        heights = jax.random.uniform(jax.random.fold_in(jax.random.fold_in(key, 6), position), (shards_of,), jnp.float32, least / len(split), top_value / len(split))
        gain = gain * jnp.repeat(jnp.exp(heights), dims[position] // shards_of).reshape((-1,) + (1,) * (len(dims) - 1 - position))
    return gain


def centred(rng, extent, width, limit, pieces=(), kind=jnp.bfloat16):
    level = levels(rng, extent, pieces, -0.22, 0.18) if pieces else 1.0
    entries = jax.random.normal(rng, extent, jnp.float32) * width * level
    return jnp.minimum(jnp.maximum(entries, -limit), limit).astype(kind)


def setup_inputs(seed: int = 0) -> dict:
    streams_of = jax.random.split(jax.random.key(seed), 10)
    return {
        "query_rows": draw_query_rows(jax.random.fold_in(streams_of[9], 71), 0),
        "key_rows": draw_key_rows(jax.random.fold_in(streams_of[9], 71), 0),
        "value_rows": centred(streams_of[2], (SEQUENCE_TOKENS, HA * HD), 1.0, 5.0, ((0, 32),)),
        "ssd_input": centred(streams_of[3], (SEQUENCE_TOKENS, SPACE_HEADS * SSD_HEAD_DIM), 1.0, 5.0, ((0, 32),)),
        "state_write": centred(streams_of[4], (SEQUENCE_TOKENS, GROUPS * STATE), STATE ** -0.5, 0.5, ((0, 32),)),
        "state_read": centred(streams_of[5], (SEQUENCE_TOKENS, GROUPS * STATE), SEQUENCE_TOKENS ** -0.5, 0.125, ((0, 32),)),
        "step_size": jnp.clip(jnp.exp(math.log(1.0) - 1.3862944 * jax.random.uniform(streams_of[6], (SEQUENCE_TOKENS, SPACE_HEADS), jnp.float32) ** levels(streams_of[6], (SEQUENCE_TOKENS, SPACE_HEADS), ((0, 32),), -0.2, 0.2)), 0.25, 1.0).astype(jnp.bfloat16),
        "decay_log": draw_decay_log(jax.random.fold_in(streams_of[9], 71), 0),
        "skip_gain": jnp.clip(0.1 + 0.4 * jax.random.uniform(streams_of[8], (SPACE_HEADS,), jnp.float32) ** levels(streams_of[8], (SPACE_HEADS,), ((0, 4),), -0.2, 0.2), 0.1, 0.5),
    }


exact_mode = lax.Precision.HIGHEST


def stretch_terms(state, x_block, dt_block, log_block, write_block, read_block):
    step_vals = dt_block.astype(jnp.float32)
    log_vals = log_block.astype(jnp.float32)
    cumulated = jnp.cumsum(log_vals, axis=0)
    driven = x_block.astype(jnp.float32) * step_vals[:, :, None]
    per_group = x_block.shape[1] // write_block.shape[1]
    write_f = write_block.astype(jnp.float32)
    read_f = read_block.astype(jnp.float32)
    write_heads = jnp.repeat(write_f, per_group, axis=1)
    read_heads = jnp.repeat(read_f, per_group, axis=1)
    intersection = jnp.einsum("ign,jgn->gij", read_f, write_f, precision=exact_mode)
    intersection = jnp.repeat(intersection, per_group, axis=0)
    length = log_vals.shape[0]
    causal = (jnp.arange(length)[:, None] >= jnp.arange(length)[None, :])[None]
    cum_heads = cumulated.T
    log_gaps = cum_heads[:, :, None] - cum_heads[:, None, :]
    weights = jnp.where(causal, jnp.exp(jnp.where(causal, log_gaps, 0.0)), 0.0)
    output = jnp.einsum("hij,jhp->ihp", intersection * weights, driven, precision=exact_mode)
    output = output + jnp.exp(cumulated)[:, :, None] * jnp.einsum("ihn,hpn->ihp", read_heads, state, precision=exact_mode)
    final_log = cumulated[-1]
    scaled = driven * jnp.exp(final_log[None, :] - cumulated)[:, :, None]
    carried = jnp.exp(final_log)[:, None, None] * state + jnp.einsum("jhp,jhn->hpn", scaled, write_heads, precision=exact_mode)
    return output, carried


def attend_block(index, query_rows, padded_keys, padded_values, span):
    start = (index * STRETCH).astype(jnp.int32)
    query_block = lax.dynamic_slice_in_dim(query_rows, start, STRETCH, 0)
    key_block = lax.dynamic_slice_in_dim(padded_keys, start, span + STRETCH, 0)
    value_block = lax.dynamic_slice_in_dim(padded_values, start, span + STRETCH, 0)
    query_f = query_block.reshape(STRETCH, HA, HD).astype(jnp.float32)
    key_f = key_block.reshape(span + STRETCH, HA, HD).astype(jnp.float32)
    value_f = value_block.reshape(span + STRETCH, HA, HD).astype(jnp.float32)
    scores = jnp.einsum("qhd,khd->hqk", query_f, key_f) * (1.0 / (HD ** 0.5))
    query_pos = jnp.arange(STRETCH)[:, None]
    key_pos = jnp.arange(span + STRETCH)[None, :]
    valid = (key_pos > query_pos) & (key_pos <= query_pos + span) & (key_pos + index * STRETCH >= span)
    scores = jnp.where(valid[None], scores, -1e30)
    top_score = jnp.max(scores, axis=2, keepdims=True)
    expo = jnp.exp(scores - top_score)
    probs = (expo / jnp.sum(expo, axis=2, keepdims=True)).astype(jnp.bfloat16)
    result = jnp.einsum("hqk,khd->qhd", probs.astype(jnp.float32), value_f)
    return result.astype(jnp.bfloat16).reshape(STRETCH, HA * HD)


def reference(query_rows, key_rows, value_rows, ssd_input, state_write, state_read, step_size, decay_log, skip_gain):
    span = REACH * BLOCK_LEN
    front = jnp.zeros((span, HA * HD), jnp.bfloat16)
    padded_keys = jnp.concatenate([front, key_rows], axis=0)
    padded_values = jnp.concatenate([front, value_rows], axis=0)
    blocks = lax.map(lambda index: attend_block(index, query_rows, padded_keys, padded_values, span), jnp.arange(SEQUENCE_TOKENS // STRETCH, dtype=jnp.int32))
    attended = blocks.reshape(SEQUENCE_TOKENS, HA * HD)
    count = SEQUENCE_TOKENS // STRETCH
    x_all = ssd_input.reshape(count, STRETCH, SPACE_HEADS, SSD_HEAD_DIM)
    dt_all = step_size.reshape(count, STRETCH, SPACE_HEADS)
    log_all = decay_log.reshape(count, STRETCH, SPACE_HEADS)
    write_all = state_write.reshape(count, STRETCH, GROUPS, STATE)
    read_all = state_read.reshape(count, STRETCH, GROUPS, STATE)

    def advance(state, inputs):
        output, carried = stretch_terms(state, *inputs)
        return carried, output

    initial = jnp.zeros((SPACE_HEADS, SSD_HEAD_DIM, STATE), jnp.float32)
    final_state, outputs = lax.scan(advance, initial, (x_all, dt_all, log_all, write_all, read_all))
    outputs = outputs.reshape(SEQUENCE_TOKENS, SPACE_HEADS, SSD_HEAD_DIM)
    outputs = outputs + skip_gain[None, :, None] * ssd_input.reshape(SEQUENCE_TOKENS, SPACE_HEADS, SSD_HEAD_DIM).astype(jnp.float32)
    scanned = outputs.astype(jnp.bfloat16).reshape(SEQUENCE_TOKENS, SPACE_HEADS * SSD_HEAD_DIM)
    return attended, scanned
```

```python
import functools
import math

import jax
import jax.numpy as jnp
import numpy as np
from jax import lax
from jax.experimental import pallas as pl
from jax.experimental.pallas import tpu as pltpu
from jax.sharding import Mesh, PartitionSpec as P


HA = 64
HD = 128
SPACE_HEADS = 128
SSD_HEAD_DIM = 64
STATE = 128
GROUPS = 8
REACH = 4

SPLIT = True
CHUNKS = 2
TILE = 256
SCAN = 128
FAR = -1e30
LOG2 = math.log2(math.e) / math.sqrt(HD)
PLANE = ("core", "head")
VMEM = pl.BlockSpec(memory_space=pltpu.VMEM)
SMEM = pl.BlockSpec(memory_space=pltpu.SMEM)
F32, BF16 = jnp.float32, jnp.bfloat16
PARAMS = pltpu.CompilerParams(vmem_limit_bytes=32 * 2**20)


def dot(a, b, ca=1, cb=0, precision=None):
    return lax.dot_general(
        a, b, (((ca,), (cb,)), ((), ())), preferred_element_type=F32, precision=precision
    )


def split3(v):
    hi = v.astype(BF16)
    rest = v - hi.astype(F32)
    mid = rest.astype(BF16)
    low = (rest - mid.astype(F32)).astype(BF16)
    return hi, mid, low


def block_of(slot, heads_axis):
    return (slot % heads_axis) * 2 + slot // heads_axis


def pack_kernel(maps, widths, *refs):
    ins, out, sems = refs[: len(maps)], refs[-2], refs[-1]
    copies = []
    for s in range(out.shape[0]):
        at = 0
        for n, (ref, place, width) in enumerate(zip(ins, maps, widths)):
            copies.append(
                pltpu.make_async_copy(
                    ref.at[:, pl.ds(place(s) * width, width)],
                    out.at[s, :, pl.ds(at, width)],
                    sems.at[s, n],
                )
            )
            at += width
    for copy in copies:
        copy.start()
    for copy in copies:
        copy.wait()


def pack(arrays, widths, maps, slots):
    tokens = arrays[0].shape[0]
    total = sum(widths)
    return pl.pallas_call(
        functools.partial(pack_kernel, maps, widths),
        in_specs=[pl.BlockSpec(memory_space=pltpu.HBM)] * len(arrays),
        out_specs=pl.BlockSpec(memory_space=pltpu.VMEM),
        out_shape=jax.ShapeDtypeStruct((slots, tokens, total), BF16),
        scratch_shapes=[pltpu.SemaphoreType.DMA((slots, len(arrays)))],
    )(*arrays)


def pack_scan_kernel(maps, widths, local, *refs):
    count = len(maps)
    step_ref, log_ref, out, sems = refs[count:]
    copies = []
    for s in range(out.shape[0]):
        at = 0
        for n, (place, width) in enumerate(zip(maps, widths)):
            copies.append(
                pltpu.make_async_copy(
                    refs[n].at[:, pl.ds(place(s) * width, width)],
                    out.at[s, :, pl.ds(at, width)],
                    sems.at[s, n],
                )
            )
            at += width
    for copy in copies:
        copy.start()
    row = lax.broadcasted_iota(jnp.int32, (SPACE_HEADS, SPACE_HEADS), 0)
    column = lax.broadcasted_iota(jnp.int32, (SPACE_HEADS, SPACE_HEADS), 1)
    for s in range(out.shape[0]):
        first = maps[0](s) * local
        steps = ((column < local) & (row == first + column)).astype(BF16)
        logs = (column >= local) & (column < 2 * local) & (row == first + column - local)
        both = dot(step_ref[...], steps) + dot(log_ref[...], logs.astype(BF16))
        out[s, :, sum(widths) :] = both.astype(BF16)
    for copy in copies:
        copy.wait()


def pack_scan(arrays, widths, maps, local, slots):
    tokens = arrays[0].shape[0]
    total = sum(widths) + SPACE_HEADS
    return pl.pallas_call(
        functools.partial(pack_scan_kernel, maps, widths, local),
        in_specs=[pl.BlockSpec(memory_space=pltpu.HBM)] * len(widths) + [VMEM, VMEM],
        out_specs=VMEM,
        out_shape=jax.ShapeDtypeStruct((slots, tokens, total), BF16),
        scratch_shapes=[pltpu.SemaphoreType.DMA((slots, len(widths)))],
    )(*arrays)


def unpack_kernel(heads_axis, *refs):
    parts, out, sems = refs[:-2], refs[-2], refs[-1]
    slots = parts[0].shape[0]
    copies = []
    for s in range(slots):
        at = block_of(s, heads_axis) * (out.shape[1] // slots)
        for n, part in enumerate(parts):
            width = part.shape[2]
            copies.append(
                pltpu.make_async_copy(part.at[s], out.at[:, pl.ds(at, width)], sems.at[s, n])
            )
            at += width
    for copy in copies:
        copy.start()
    for copy in copies:
        copy.wait()


def unpack(parts, heads_axis):
    slots, tokens, _ = parts[0].shape
    total = sum(p.shape[2] for p in parts)
    return pl.pallas_call(
        functools.partial(unpack_kernel, heads_axis),
        in_specs=[pl.BlockSpec(memory_space=pl.ANY)] * len(parts),
        out_specs=pl.BlockSpec(memory_space=pltpu.VMEM),
        out_shape=jax.ShapeDtypeStruct((tokens, total * slots), BF16),
        scratch_shapes=[pltpu.SemaphoreType.DMA((slots, len(parts)))],
        compiler_params=PARAMS,
    )(*parts)


def exchange(sent):
    return lax.all_to_all(sent, PLANE, split_axis=0, concat_axis=0, tiled=True)


def shift(value, distance):
    count = lax.axis_size("z")
    route = [(i, i + distance) for i in range(count) if 0 <= i + distance < count]
    return lax.ppermute(value, "z", route)


def with_ones(v):
    return jnp.concatenate([v, jnp.ones((v.shape[0], HD), BF16)], axis=1)


def diagonal():
    return lax.broadcasted_iota(jnp.int32, (HD, HD), 0) == lax.broadcasted_iota(
        jnp.int32, (HD, HD), 1
    )


def over_heads(heads, run):
    if heads <= 4:
        for head in range(heads):
            run(head, head * HD)
        return

    def some(index, carry):
        for n in range(2):
            run(None, pl.multiple_of((index * 2 + n) * HD, HD))
        return carry

    lax.fori_loop(0, heads // 2, some, 0)


def flat(ref):
    return ref.reshape(ref.shape[0] * ref.shape[1], ref.shape[2])


def attend_kernel(mode, q_head, kv_head, heads, place, q_ref, kv_ref, *refs):
    came_ref, out_ref = (refs[0], refs[1]) if mode != "far" else (None, refs[0])
    q_ref, kv_ref = flat(q_ref), flat(kv_ref)
    if mode == "own":
        out_ref = flat(out_ref)
    rows = q_ref.shape[0]
    side = heads * HD
    pieces = rows // HD
    bias = jnp.where(place[0] > 0, 0.0, FAR).astype(F32)
    tile = min(TILE, rows)
    row = lax.broadcasted_iota(jnp.int32, (tile, tile), 0)
    column = lax.broadcasted_iota(jnp.int32, (tile, tile), 1)
    seen = row >= column if mode == "own" else row < column
    unit = diagonal()
    used = rows + 3 * pieces
    if mode != "own" and used < out_ref.shape[0]:
        out_ref[used:] = jnp.zeros((out_ref.shape[0] - used, side), BF16)
    if came_ref is not None:
        tail = came_ref[rows:].astype(F32)
        tail = sum(tail[n * pieces : (n + 1) * pieces] for n in range(3)) + bias
        lines = [tail[:, h * HD : (h + 1) * HD] for h in range(heads)]
        lines.append(jnp.zeros((HD - heads * pieces, HD), F32))
        came_lse = jnp.concatenate(lines, axis=0).T

    def run(head, lane):
        at = pl.ds(lane, HD)
        q_at = pl.ds(q_head * HD + lane, HD)
        k_at = pl.ds(kv_head * HD + lane, HD)
        v = with_ones(kv_ref[:, pl.ds(kv_ref.shape[1] // 2 + kv_head * HD + lane, HD)])
        for start in range(0, rows, tile):
            end = start + tile
            q = q_ref[start:end, q_at]
            spans = {"own": (0, start), "next": (0, rows), "far": (end, rows)}[mode]
            parts = []
            if spans[1] > spans[0]:
                span = slice(*spans)
                parts.append((dot(q, kv_ref[span, k_at], 1, 1), span))
            if mode != "next":
                span = slice(start, end)
                masked = jnp.where(seen, dot(q, kv_ref[span, k_at], 1, 1), FAR)
                parts.append((masked, span))
            tops = [jnp.max(s, axis=1, keepdims=True) for s, _ in parts]
            top = jnp.broadcast_to(functools.reduce(jnp.maximum, tops) * LOG2, (tile, HD))
            if came_ref is not None:
                first = head * pieces + start // HD
                other = [
                    jnp.broadcast_to(came_lse[:, first + n : first + n + 1], (HD, HD))
                    for n in range(tile // HD)
                ]
                other = jnp.concatenate(other, axis=0)
                top = jnp.maximum(top, other)
            both = None
            for s, span in parts:
                lanes = range(0, s.shape[1], HD)
                expo = [jnp.exp2(s[:, n : n + HD] * LOG2 - top).astype(BF16) for n in lanes]
                share = dot(jnp.concatenate(expo, axis=1), v[span])
                both = share if both is None else both + share
            result, total = both[:, :HD], both[:, HD:]
            if came_ref is not None:
                weight = jnp.exp2(other - top)
                result = result + weight * came_ref[start:end, at].astype(F32)
                total = total + weight
            out_ref[start:end, at] = (result / total).astype(BF16)
            if mode != "own":
                lse = top + jnp.log2(total)
                for piece in range(0, tile, HD):
                    kept = jnp.where(unit, lse[piece : piece + HD], 0.0)
                    line = jnp.sum(kept, axis=0, keepdims=True)
                    for n, part in enumerate(split3(line)):
                        there = rows + n * pieces + (start + piece) // HD
                        out_ref[there : there + 1, at] = part

    over_heads(heads, run)


def cost(flops, size):
    return pl.CostEstimate(flops=flops, bytes_accessed=size, transcendentals=0)


def attend(mode, place, query, q_head, kv, kv_head, heads, came=()):
    slots, tokens, _ = query.shape
    rows = slots * tokens
    tall = (rows + -(-3 * (rows // HD) // 16) * 16,)
    if mode == "own":
        tall = (slots, tokens)
    return pl.pallas_call(
        functools.partial(attend_kernel, mode, q_head, kv_head, heads),
        in_specs=[SMEM, VMEM, VMEM] + [VMEM] * len(came),
        out_specs=VMEM,
        out_shape=jax.ShapeDtypeStruct(tall + (heads * HD,), BF16),
        compiler_params=PARAMS,
        cost_estimate=cost(4 * rows * rows * HD * heads, 8 * rows * HD * heads),
    )(place, query, kv, *came)


def chosen(shape, width, first):
    row = lax.broadcasted_iota(jnp.int32, shape, 0)
    column = lax.broadcasted_iota(jnp.int32, shape, 1)
    return (row == first + column // width).astype(BF16)


def parts_of(ref, width, rows=slice(None)):
    edges = [0, width, width + STATE, width + 2 * STATE]
    x = ref[rows, 0:width]
    write = ref[rows, edges[1] : edges[2]]
    read = ref[rows, edges[2] : edges[3]]
    return x, write, read, ref[rows, edges[3] :]


def pack_state(sent_ref, state, logs):
    width = state.shape[1]
    sent_ref[0:STATE] = state.astype(BF16)
    tail = [p.astype(F32) for p in split3(logs)] + [jnp.zeros((13, width), F32)]
    sent_ref[STATE:] = jnp.concatenate(tail, axis=0).astype(BF16)


def came_state(ref):
    tail = ref[STATE:].astype(F32)
    return ref[0:STATE].astype(F32), tail[0:1] + tail[1:2] + tail[2:3]


def end_kernel(width, ref, sent_ref):
    ref = flat(ref)
    rows = ref.shape[0]
    local = width // SSD_HEAD_DIM
    step_spread = chosen((SPACE_HEADS, width), SSD_HEAD_DIM, 0)
    log_spread = chosen((SPACE_HEADS, width), SSD_HEAD_DIM, local)
    tile = min(256, rows)
    after = lax.broadcasted_iota(jnp.int32, (tile, tile), 0) < lax.broadcasted_iota(
        jnp.int32, (tile, tile), 1
    )
    after = after.astype(BF16)
    state = jnp.zeros((STATE, width), F32)
    behind = jnp.zeros((1, width), F32)
    for start in reversed(range(0, rows, tile)):
        x, write, _, both = parts_of(ref, width, slice(start, start + tile))
        log_wide = dot(both, log_spread).astype(BF16)
        suffix = dot(after, log_wide) + behind
        weighed = x.astype(F32) * dot(both, step_spread) * jnp.exp(suffix)
        state += dot(write, weighed.astype(BF16), 0, 0)
        behind = suffix[0:1] + log_wide[0:1].astype(F32)
    pack_state(sent_ref, state, behind)


def state_shape(width):
    return jax.ShapeDtypeStruct((STATE + 16, width), BF16)


def end_state(recv, width):
    rows = recv.shape[0] * recv.shape[1]
    return pl.pallas_call(
        functools.partial(end_kernel, width),
        in_specs=[VMEM],
        out_specs=VMEM,
        out_shape=state_shape(width),
        compiler_params=PARAMS,
        cost_estimate=cost(2 * rows * width * 1024, 2 * rows * width),
    )(recv)


def join_kernel(own_ref, came_ref, sent_ref):
    state, logs = came_state(came_ref)
    own, own_logs = came_state(own_ref)
    pack_state(sent_ref, own + jnp.exp(own_logs) * state, own_logs + logs)


def join_state(own, came):
    return pl.pallas_call(
        join_kernel,
        in_specs=[VMEM, VMEM],
        out_specs=VMEM,
        out_shape=state_shape(own.shape[1]),
        compiler_params=PARAMS,
        cost_estimate=cost(own.size * 100, 8 * own.size),
    )(own, came)


def local_kernel(width, ref, gain_ref, out_ref, fade_ref, state_ref, passed_ref):
    ref = flat(ref)
    rows = ref.shape[0]
    local = width // SSD_HEAD_DIM
    step_spread = chosen((SPACE_HEADS, width), SSD_HEAD_DIM, 0)
    log_spread = chosen((SPACE_HEADS, width), SSD_HEAD_DIM, local)
    picked = chosen((SPACE_HEADS, SPACE_HEADS), 1, local)
    size = min(SCAN, rows)
    row = lax.broadcasted_iota(jnp.int32, (size, size), 0)
    column = lax.broadcasted_iota(jnp.int32, (size, size), 1)
    causal = row >= column
    lower = causal.astype(BF16)
    unit = (row == column).astype(BF16)
    left = lax.broadcasted_iota(jnp.int32, (size, HD), 1) < SSD_HEAD_DIM
    state_ref[...] = jnp.zeros((STATE, width), F32)
    passed_ref[...] = jnp.zeros((8, width), F32)

    def step_of(index, _):
        here = pl.ds(pl.multiple_of(index * size, size), size)
        x, write, read, both = parts_of(ref, width, here)
        step_wide = dot(both, step_spread)
        cum = dot(lower, dot(both, log_spread).astype(BF16))
        log_pick = dot(both, picked).astype(BF16)
        cum_pick = dot(lower, log_pick)
        cum_rows = dot(log_pick, lower, 0, 1)
        step_rows = dot(both, unit, 0, 0)
        mixing = dot(read, write, 1, 1)
        state = state_ref[...]
        base = jnp.exp(cum) * dot(read, state.astype(BF16))
        base += gain_ref[...] * x.astype(F32)
        for pair in range(0, local, 2):
            lanes = slice(pair * SSD_HEAD_DIM, pair * SSD_HEAD_DIM + HD)
            halves = []
            for h in (pair, pair + 1):
                gap = cum_pick[:, h : h + 1] - cum_rows[h : h + 1, :]
                weight = jnp.exp(jnp.where(causal, gap, FAR)) * (mixing * step_rows[h : h + 1, :])
                halves.append(dot(weight.astype(BF16), x[:, lanes]))
            total = base[:, lanes] + jnp.where(left, halves[0], halves[1])
            out_ref[here, lanes] = total
        passed = passed_ref[0:1]
        fade_ref[here] = jnp.exp(passed + cum).astype(BF16)
        last = cum[size - 1 : size]
        passed_ref[...] = jnp.broadcast_to(passed + last, (8, width))
        weighed = x.astype(F32) * step_wide * jnp.exp(last - cum)
        state_ref[...] = jnp.exp(last) * state + dot(write, weighed.astype(BF16), 0, 0)
        return _

    lax.fori_loop(0, rows // size, step_of, 0)


def local_scan(recv, gain, width):
    rows = recv.shape[0] * recv.shape[1]
    return pl.pallas_call(
        functools.partial(local_kernel, width),
        in_specs=[VMEM, VMEM],
        out_specs=[VMEM, VMEM],
        out_shape=[
            jax.ShapeDtypeStruct((rows, width), F32),
            jax.ShapeDtypeStruct((rows, width), BF16),
        ],
        scratch_shapes=[pltpu.VMEM((STATE, width), F32), pltpu.VMEM((8, width), F32)],
        compiler_params=PARAMS,
        cost_estimate=cost(2 * rows * width * 1024, 4 * rows * width),
    )(recv, gain)


def enter_kernel(width, ref, local_ref, fade_ref, *refs):
    came, out_ref, ref = refs[:-1], flat(refs[-1]), flat(ref)
    entry, behind = jnp.zeros((STATE, width), F32), jnp.zeros((1, width), F32)
    for one in came:
        state, passed = came_state(one)
        entry += jnp.exp(behind) * state
        behind += passed
    entry = entry.astype(BF16)
    size = min(SCAN, out_ref.shape[0])
    for start in range(0, out_ref.shape[0], size):
        here = slice(start, start + size)
        read = parts_of(ref, width, here)[2]
        total = local_ref[here] + fade_ref[here].astype(F32) * dot(read, entry)
        out_ref[here] = total.astype(BF16)


def enter(recv, local, fade, came, width):
    rows = recv.shape[0] * recv.shape[1]
    return pl.pallas_call(
        functools.partial(enter_kernel, width),
        in_specs=[VMEM] * (3 + len(came)),
        out_specs=VMEM,
        out_shape=jax.ShapeDtypeStruct(recv.shape[:2] + (width,), BF16),
        compiler_params=PARAMS,
        cost_estimate=cost(2 * rows * width * 128, 9 * rows * width),
    )(recv, local, fade, *came)


def body(q, k, v, x, write, read, step, logs, gain):
    heads_axis = lax.axis_size("head")
    slots = 2 * heads_axis
    heads = HA // slots
    chunks = min(CHUNKS, heads)
    per = heads // chunks
    width = SPACE_HEADS * SSD_HEAD_DIM // slots
    place = lax.axis_index("z").astype(jnp.int32).reshape(1)
    core = lax.axis_index("core")

    def block(s):
        return block_of(s, heads_axis)

    def heads_in(arrays, c, count):
        at = lambda s: block(s) * count + c
        wide = heads * HD // count
        sent = pack(arrays, (wide,) * len(arrays), (at,) * len(arrays), slots)
        return exchange(sent)

    each = range(chunks)
    whole = heads_in((q,), 0, 1)
    query = [whole[:, :, c * per * HD : (c + 1) * per * HD] for c in each]
    below, lower = [], []
    for c in each:
        below.append(shift(query[c], -1))
        lower.append(shift(below[c], -1))

    group = lambda s: block(s) * GROUPS // slots
    local = width // SSD_HEAD_DIM
    sent = pack_scan(
        (x, write, read, step, logs), (width, STATE, STATE), (block, group, group), local, slots
    )
    recv = exchange(sent)
    if SPLIT:
        kv = [(heads_in((k, v), c, chunks), 0) for c in each]
    else:
        joint = heads_in((k, v), 0, 1)
        kv = [(joint, c * per) for c in each]
    sent = end_state(recv, width)
    came = [shift(sent, 1)]
    reach = 2
    while reach < lax.axis_size("z"):
        sent = join_state(sent, came[-1])
        came.append(shift(sent, reach))
        reach *= 2
    own_gain = lax.dynamic_slice_in_dim(gain, core * local, local, 0)
    wide_gain = jnp.repeat(own_gain, SSD_HEAD_DIM)[None, :]
    within, fade = local_scan(recv, wide_gain, width)
    scanned = enter(recv, within, fade, came, width)
    scanned = exchange(scanned)

    attended = []
    for c in each:
        partial = attend("far", place, lower[c], 0, *kv[c], per)
        partial = shift(partial, 1)
        partial = attend("next", place, below[c], 0, *kv[c], per, (partial,))
        partial = shift(partial, 1)
        mixed = attend("own", place, whole, c * per, *kv[c], per, (partial,))
        attended.append(exchange(mixed))
    return unpack(attended, heads_axis), unpack([scanned], heads_axis)


def solution(mesh):
    ctx, heads_axis = mesh.shape["ctx"], mesh.shape["head"]
    assert REACH == 4 and ctx % 2 == 0 and (2 * heads_axis) % GROUPS == 0
    cut = Mesh(np.asarray(mesh.devices).reshape(ctx // 2, 2, heads_axis), ("z", "core", "head"))
    rows = P(("z", "core", "head"), None)
    return jax.shard_map(
        body,
        mesh=cut,
        in_specs=(rows,) * 8 + (P("head"),),
        out_specs=(rows, rows),
        check_vma=False,
    )
```

```python
import functools
import math

import jax
import jax.numpy as jnp
import numpy as np
from jax import lax
from jax.experimental import pallas as pl
from jax.experimental.pallas import tpu as pltpu
from jax.sharding import Mesh, PartitionSpec as P


HA = 64
HD = 128
SPACE_HEADS = 128
SSD_HEAD_DIM = 64
STATE = 128
GROUPS = 8
REACH = 4

SPLIT = True
CHUNKS = 2
TILE = 256
SCAN = 128
FAR = -1e30
LOG2 = math.log2(math.e) / math.sqrt(HD)
PLANE = ("core", "head")
VMEM = pl.BlockSpec(memory_space=pltpu.VMEM)
SMEM = pl.BlockSpec(memory_space=pltpu.SMEM)
F32, BF16 = jnp.float32, jnp.bfloat16
PARAMS = pltpu.CompilerParams(vmem_limit_bytes=32 * 2**20)


def dot(a, b, ca=1, cb=0, precision=None):
    return lax.dot_general(
        a, b, (((ca,), (cb,)), ((), ())), preferred_element_type=F32, precision=precision
    )


def split3(v):
    hi = v.astype(BF16)
    rest = v - hi.astype(F32)
    mid = rest.astype(BF16)
    low = (rest - mid.astype(F32)).astype(BF16)
    return hi, mid, low


def block_of(slot, heads_axis):
    return (slot % heads_axis) * 2 + slot // heads_axis


def pack_kernel(maps, widths, *refs):
    ins, out, sems = refs[: len(maps)], refs[-2], refs[-1]
    copies = []
    for s in range(out.shape[0]):
        at = 0
        for n, (ref, place, width) in enumerate(zip(ins, maps, widths)):
            copies.append(
                pltpu.make_async_copy(
                    ref.at[:, pl.ds(place(s) * width, width)],
                    out.at[s, :, pl.ds(at, width)],
                    sems.at[s, n],
                )
            )
            at += width
    for copy in copies:
        copy.start()
    for copy in copies:
        copy.wait()


def pack(arrays, widths, maps, slots):
    tokens = arrays[0].shape[0]
    total = sum(widths)
    return pl.pallas_call(
        functools.partial(pack_kernel, maps, widths),
        in_specs=[pl.BlockSpec(memory_space=pltpu.HBM)] * len(arrays),
        out_specs=pl.BlockSpec(memory_space=pltpu.VMEM),
        out_shape=jax.ShapeDtypeStruct((slots, tokens, total), BF16),
        scratch_shapes=[pltpu.SemaphoreType.DMA((slots, len(arrays)))],
    )(*arrays)


def pack_scan_kernel(maps, widths, local, *refs):
    count = len(maps)
    step_ref, log_ref, out, sems = refs[count:]
    copies = []
    for s in range(out.shape[0]):
        at = 0
        for n, (place, width) in enumerate(zip(maps, widths)):
            copies.append(
                pltpu.make_async_copy(
                    refs[n].at[:, pl.ds(place(s) * width, width)],
                    out.at[s, :, pl.ds(at, width)],
                    sems.at[s, n],
                )
            )
            at += width
    for copy in copies:
        copy.start()
    row = lax.broadcasted_iota(jnp.int32, (SPACE_HEADS, SPACE_HEADS), 0)
    column = lax.broadcasted_iota(jnp.int32, (SPACE_HEADS, SPACE_HEADS), 1)
    for s in range(out.shape[0]):
        first = maps[0](s) * local
        steps = ((column < local) & (row == first + column)).astype(BF16)
        logs = (column >= local) & (column < 2 * local) & (row == first + column - local)
        both = dot(step_ref[...], steps) + dot(log_ref[...], logs.astype(BF16))
        out[s, :, sum(widths) :] = both.astype(BF16)
    for copy in copies:
        copy.wait()


def pack_scan(arrays, widths, maps, local, slots):
    tokens = arrays[0].shape[0]
    total = sum(widths) + SPACE_HEADS
    return pl.pallas_call(
        functools.partial(pack_scan_kernel, maps, widths, local),
        in_specs=[pl.BlockSpec(memory_space=pltpu.HBM)] * len(widths) + [VMEM, VMEM],
        out_specs=VMEM,
        out_shape=jax.ShapeDtypeStruct((slots, tokens, total), BF16),
        scratch_shapes=[pltpu.SemaphoreType.DMA((slots, len(widths)))],
    )(*arrays)


def unpack_kernel(chunk, chunks, heads_axis, part, *refs):
    out, sems = refs[-2:]
    slots, _, width = part.shape
    copies = []
    for s in range(slots):
        at = (block_of(s, heads_axis) * chunks + chunk) * width
        copies.append(
            pltpu.make_async_copy(part.at[s], out.at[:, pl.ds(at, width)], sems.at[s])
        )
    for copy in copies:
        copy.start()
    for copy in copies:
        copy.wait()


def unpack(parts, heads_axis):
    slots, tokens, width = parts[0].shape
    anywhere = pl.BlockSpec(memory_space=pl.ANY)
    out = ()
    for chunk, part in enumerate(parts):
        out = pl.pallas_call(
            functools.partial(unpack_kernel, chunk, len(parts), heads_axis),
            in_specs=[VMEM] + [anywhere] * len(out),
            out_specs=anywhere,
            out_shape=jax.ShapeDtypeStruct((tokens, width * slots * len(parts)), BF16),
            scratch_shapes=[pltpu.SemaphoreType.DMA((slots,))],
            input_output_aliases={1: 0} if out else {},
            compiler_params=PARAMS,
        )(part, *out)
        out = (out,)
    return out[0]


def exchange(sent):
    return lax.all_to_all(sent, PLANE, split_axis=0, concat_axis=0, tiled=True)


def shift(value, distance):
    count = lax.axis_size("z")
    route = [(i, i + distance) for i in range(count) if 0 <= i + distance < count]
    return lax.ppermute(value, "z", route)


def with_ones(v):
    return jnp.concatenate([v, jnp.ones((v.shape[0], HD), BF16)], axis=1)


def diagonal():
    return lax.broadcasted_iota(jnp.int32, (HD, HD), 0) == lax.broadcasted_iota(
        jnp.int32, (HD, HD), 1
    )


def over_heads(heads, run):
    if heads <= 4:
        for head in range(heads):
            run(head, head * HD)
        return

    def some(index, carry):
        for n in range(2):
            run(None, pl.multiple_of((index * 2 + n) * HD, HD))
        return carry

    lax.fori_loop(0, heads // 2, some, 0)


def flat(ref):
    return ref.reshape(ref.shape[0] * ref.shape[1], ref.shape[2])


def attend_kernel(mode, q_head, kv_head, heads, place, q_ref, kv_ref, *refs):
    came_ref, out_ref = (refs[0], refs[1]) if mode != "far" else (None, refs[0])
    q_ref, kv_ref = flat(q_ref), flat(kv_ref)
    if mode == "own":
        out_ref = flat(out_ref)
    rows = q_ref.shape[0]
    side = heads * HD
    pieces = rows // HD
    bias = jnp.where(place[0] > 0, 0.0, FAR).astype(F32)
    tile = min(TILE, rows)
    row = lax.broadcasted_iota(jnp.int32, (tile, tile), 0)
    column = lax.broadcasted_iota(jnp.int32, (tile, tile), 1)
    seen = row >= column if mode == "own" else row < column
    unit = diagonal()
    used = rows + 3 * pieces
    if mode != "own" and used < out_ref.shape[0]:
        out_ref[used:] = jnp.zeros((out_ref.shape[0] - used, side), BF16)
    if came_ref is not None:
        tail = came_ref[rows:].astype(F32)
        tail = sum(tail[n * pieces : (n + 1) * pieces] for n in range(3)) + bias
        lines = [tail[:, h * HD : (h + 1) * HD] for h in range(heads)]
        lines.append(jnp.zeros((HD - heads * pieces, HD), F32))
        came_lse = jnp.concatenate(lines, axis=0).T

    def run(head, lane):
        at = pl.ds(lane, HD)
        q_at = pl.ds(q_head * HD + lane, HD)
        k_at = pl.ds(kv_head * HD + lane, HD)
        v = with_ones(kv_ref[:, pl.ds(kv_ref.shape[1] // 2 + kv_head * HD + lane, HD)])
        for start in range(0, rows, tile):
            end = start + tile
            q = q_ref[start:end, q_at]
            spans = {"own": (0, start), "next": (0, rows), "far": (end, rows)}[mode]
            parts = []
            if spans[1] > spans[0]:
                span = slice(*spans)
                parts.append((dot(q, kv_ref[span, k_at], 1, 1), span))
            if mode != "next":
                span = slice(start, end)
                masked = jnp.where(seen, dot(q, kv_ref[span, k_at], 1, 1), FAR)
                parts.append((masked, span))
            tops = [jnp.max(s, axis=1, keepdims=True) for s, _ in parts]
            top = jnp.broadcast_to(functools.reduce(jnp.maximum, tops) * LOG2, (tile, HD))
            if came_ref is not None:
                first = head * pieces + start // HD
                other = [
                    jnp.broadcast_to(came_lse[:, first + n : first + n + 1], (HD, HD))
                    for n in range(tile // HD)
                ]
                other = jnp.concatenate(other, axis=0)
                top = jnp.maximum(top, other)
            both = None
            for s, span in parts:
                lanes = range(0, s.shape[1], HD)
                expo = [jnp.exp2(s[:, n : n + HD] * LOG2 - top).astype(BF16) for n in lanes]
                share = dot(jnp.concatenate(expo, axis=1), v[span])
                both = share if both is None else both + share
            result, total = both[:, :HD], both[:, HD:]
            if came_ref is not None:
                weight = jnp.exp2(other - top)
                result = result + weight * came_ref[start:end, at].astype(F32)
                total = total + weight
            out_ref[start:end, at] = (result / total).astype(BF16)
            if mode != "own":
                lse = top + jnp.log2(total)
                for piece in range(0, tile, HD):
                    kept = jnp.where(unit, lse[piece : piece + HD], 0.0)
                    line = jnp.sum(kept, axis=0, keepdims=True)
                    for n, part in enumerate(split3(line)):
                        there = rows + n * pieces + (start + piece) // HD
                        out_ref[there : there + 1, at] = part

    over_heads(heads, run)


def cost(flops, size):
    return pl.CostEstimate(flops=flops, bytes_accessed=size, transcendentals=0)


def attend(mode, place, query, q_head, kv, kv_head, heads, came=()):
    slots, tokens, _ = query.shape
    rows = slots * tokens
    tall = (rows + -(-3 * (rows // HD) // 16) * 16,)
    if mode == "own":
        tall = (slots, tokens)
    return pl.pallas_call(
        functools.partial(attend_kernel, mode, q_head, kv_head, heads),
        in_specs=[SMEM, VMEM, VMEM] + [VMEM] * len(came),
        out_specs=VMEM,
        out_shape=jax.ShapeDtypeStruct(tall + (heads * HD,), BF16),
        compiler_params=PARAMS,
        cost_estimate=cost(4 * rows * rows * HD * heads, 8 * rows * HD * heads),
    )(place, query, kv, *came)


def chosen(shape, width, first):
    row = lax.broadcasted_iota(jnp.int32, shape, 0)
    column = lax.broadcasted_iota(jnp.int32, shape, 1)
    return (row == first + column // width).astype(BF16)


def parts_of(ref, width, rows=slice(None)):
    edges = [0, width, width + STATE, width + 2 * STATE]
    x = ref[rows, 0:width]
    write = ref[rows, edges[1] : edges[2]]
    read = ref[rows, edges[2] : edges[3]]
    return x, write, read, ref[rows, edges[3] :]


def pack_state(sent_ref, state, logs):
    width = state.shape[1]
    sent_ref[0:STATE] = state.astype(BF16)
    tail = [p.astype(F32) for p in split3(logs)] + [jnp.zeros((13, width), F32)]
    sent_ref[STATE:] = jnp.concatenate(tail, axis=0).astype(BF16)


def came_state(ref):
    tail = ref[STATE:].astype(F32)
    return ref[0:STATE].astype(F32), tail[0:1] + tail[1:2] + tail[2:3]


def end_kernel(width, ref, sent_ref):
    ref = flat(ref)
    rows = ref.shape[0]
    local = width // SSD_HEAD_DIM
    step_spread = chosen((SPACE_HEADS, width), SSD_HEAD_DIM, 0)
    log_spread = chosen((SPACE_HEADS, width), SSD_HEAD_DIM, local)
    tile = min(256, rows)
    after = lax.broadcasted_iota(jnp.int32, (tile, tile), 0) < lax.broadcasted_iota(
        jnp.int32, (tile, tile), 1
    )
    after = after.astype(BF16)
    state = jnp.zeros((STATE, width), F32)
    behind = jnp.zeros((1, width), F32)
    for start in reversed(range(0, rows, tile)):
        x, write, _, both = parts_of(ref, width, slice(start, start + tile))
        log_wide = dot(both, log_spread).astype(BF16)
        suffix = dot(after, log_wide) + behind
        weighed = x.astype(F32) * dot(both, step_spread) * jnp.exp(suffix)
        state += dot(write, weighed.astype(BF16), 0, 0)
        behind = suffix[0:1] + log_wide[0:1].astype(F32)
    pack_state(sent_ref, state, behind)


def state_shape(width):
    return jax.ShapeDtypeStruct((STATE + 16, width), BF16)


def end_state(recv, width):
    rows = recv.shape[0] * recv.shape[1]
    return pl.pallas_call(
        functools.partial(end_kernel, width),
        in_specs=[VMEM],
        out_specs=VMEM,
        out_shape=state_shape(width),
        compiler_params=PARAMS,
        cost_estimate=cost(2 * rows * width * 1024, 2 * rows * width),
    )(recv)


def join_kernel(own_ref, came_ref, sent_ref):
    state, logs = came_state(came_ref)
    own, own_logs = came_state(own_ref)
    pack_state(sent_ref, own + jnp.exp(own_logs) * state, own_logs + logs)


def join_state(own, came):
    return pl.pallas_call(
        join_kernel,
        in_specs=[VMEM, VMEM],
        out_specs=VMEM,
        out_shape=state_shape(own.shape[1]),
        compiler_params=PARAMS,
        cost_estimate=cost(own.size * 100, 8 * own.size),
    )(own, came)


def local_kernel(width, ref, gain_ref, out_ref, fade_ref, state_ref, passed_ref):
    ref = flat(ref)
    rows = ref.shape[0]
    local = width // SSD_HEAD_DIM
    step_spread = chosen((SPACE_HEADS, width), SSD_HEAD_DIM, 0)
    log_spread = chosen((SPACE_HEADS, width), SSD_HEAD_DIM, local)
    picked = chosen((SPACE_HEADS, SPACE_HEADS), 1, local)
    size = min(SCAN, rows)
    row = lax.broadcasted_iota(jnp.int32, (size, size), 0)
    column = lax.broadcasted_iota(jnp.int32, (size, size), 1)
    causal = row >= column
    lower = causal.astype(BF16)
    unit = (row == column).astype(BF16)
    left = lax.broadcasted_iota(jnp.int32, (size, HD), 1) < SSD_HEAD_DIM
    state_ref[...] = jnp.zeros((STATE, width), F32)
    passed_ref[...] = jnp.zeros((8, width), F32)

    def step_of(index, _):
        here = pl.ds(pl.multiple_of(index * size, size), size)
        x, write, read, both = parts_of(ref, width, here)
        step_wide = dot(both, step_spread)
        cum = dot(lower, dot(both, log_spread).astype(BF16))
        log_pick = dot(both, picked).astype(BF16)
        cum_pick = dot(lower, log_pick)
        cum_rows = dot(log_pick, lower, 0, 1)
        step_rows = dot(both, unit, 0, 0)
        mixing = dot(read, write, 1, 1)
        state = state_ref[...]
        base = jnp.exp(cum) * dot(read, state.astype(BF16))
        base += gain_ref[...] * x.astype(F32)
        for pair in range(0, local, 2):
            lanes = slice(pair * SSD_HEAD_DIM, pair * SSD_HEAD_DIM + HD)
            halves = []
            for h in (pair, pair + 1):
                gap = cum_pick[:, h : h + 1] - cum_rows[h : h + 1, :]
                weight = jnp.exp(jnp.where(causal, gap, FAR)) * (mixing * step_rows[h : h + 1, :])
                halves.append(dot(weight.astype(BF16), x[:, lanes]))
            total = base[:, lanes] + jnp.where(left, halves[0], halves[1])
            out_ref[here, lanes] = total
        passed = passed_ref[0:1]
        fade_ref[here] = jnp.exp(passed + cum).astype(BF16)
        last = cum[size - 1 : size]
        passed_ref[...] = jnp.broadcast_to(passed + last, (8, width))
        weighed = x.astype(F32) * step_wide * jnp.exp(last - cum)
        state_ref[...] = jnp.exp(last) * state + dot(write, weighed.astype(BF16), 0, 0)
        return _

    lax.fori_loop(0, rows // size, step_of, 0)


def local_scan(recv, gain, width):
    rows = recv.shape[0] * recv.shape[1]
    return pl.pallas_call(
        functools.partial(local_kernel, width),
        in_specs=[VMEM, VMEM],
        out_specs=[VMEM, VMEM],
        out_shape=[
            jax.ShapeDtypeStruct((rows, width), F32),
            jax.ShapeDtypeStruct((rows, width), BF16),
        ],
        scratch_shapes=[pltpu.VMEM((STATE, width), F32), pltpu.VMEM((8, width), F32)],
        compiler_params=PARAMS,
        cost_estimate=cost(2 * rows * width * 1024, 4 * rows * width),
    )(recv, gain)


def enter_kernel(width, ref, local_ref, fade_ref, *refs):
    came, out_ref, ref = refs[:-1], flat(refs[-1]), flat(ref)
    entry, behind = jnp.zeros((STATE, width), F32), jnp.zeros((1, width), F32)
    for one in came:
        state, passed = came_state(one)
        entry += jnp.exp(behind) * state
        behind += passed
    entry = entry.astype(BF16)
    size = min(SCAN, out_ref.shape[0])
    for start in range(0, out_ref.shape[0], size):
        here = slice(start, start + size)
        read = parts_of(ref, width, here)[2]
        total = local_ref[here] + fade_ref[here].astype(F32) * dot(read, entry)
        out_ref[here] = total.astype(BF16)


def enter(recv, local, fade, came, width):
    rows = recv.shape[0] * recv.shape[1]
    return pl.pallas_call(
        functools.partial(enter_kernel, width),
        in_specs=[VMEM] * (3 + len(came)),
        out_specs=VMEM,
        out_shape=jax.ShapeDtypeStruct(recv.shape[:2] + (width,), BF16),
        compiler_params=PARAMS,
        cost_estimate=cost(2 * rows * width * 128, 9 * rows * width),
    )(recv, local, fade, *came)


def body(q, k, v, x, write, read, step, logs, gain):
    heads_axis = lax.axis_size("head")
    slots = 2 * heads_axis
    heads = HA // slots
    chunks = min(CHUNKS, heads)
    per = heads // chunks
    width = SPACE_HEADS * SSD_HEAD_DIM // slots
    place = lax.axis_index("z").astype(jnp.int32).reshape(1)
    core = lax.axis_index("core")

    def block(s):
        return block_of(s, heads_axis)

    def heads_in(arrays, c, count):
        at = lambda s: block(s) * count + c
        wide = heads * HD // count
        sent = pack(arrays, (wide,) * len(arrays), (at,) * len(arrays), slots)
        return exchange(sent)

    each = range(chunks)
    whole = heads_in((q,), 0, 1)
    query = [whole[:, :, c * per * HD : (c + 1) * per * HD] for c in each]
    below, lower = [], []
    for c in each:
        below.append(shift(query[c], -1))
        lower.append(shift(below[c], -1))

    group = lambda s: block(s) * GROUPS // slots
    local = width // SSD_HEAD_DIM
    sent = pack_scan(
        (x, write, read, step, logs), (width, STATE, STATE), (block, group, group), local, slots
    )
    recv = exchange(sent)
    if SPLIT:
        kv = [(heads_in((k, v), c, chunks), 0) for c in each]
    else:
        joint = heads_in((k, v), 0, 1)
        kv = [(joint, c * per) for c in each]
    sent = end_state(recv, width)
    came = [shift(sent, 1)]
    reach = 2
    while reach < lax.axis_size("z"):
        sent = join_state(sent, came[-1])
        came.append(shift(sent, reach))
        reach *= 2
    own_gain = lax.dynamic_slice_in_dim(gain, core * local, local, 0)
    wide_gain = jnp.repeat(own_gain, SSD_HEAD_DIM)[None, :]
    within, fade = local_scan(recv, wide_gain, width)
    scanned = enter(recv, within, fade, came, width)
    scanned = exchange(scanned)

    attended = []
    for c in each:
        partial = attend("far", place, lower[c], 0, *kv[c], per)
        partial = shift(partial, 1)
        partial = attend("next", place, below[c], 0, *kv[c], per, (partial,))
        partial = shift(partial, 1)
        mixed = attend("own", place, whole, c * per, *kv[c], per, (partial,))
        attended.append(exchange(mixed))
    return unpack(attended, heads_axis), unpack([scanned], heads_axis)


def solution(mesh):
    ctx, heads_axis = mesh.shape["ctx"], mesh.shape["head"]
    assert REACH == 4 and ctx % 2 == 0 and (2 * heads_axis) % GROUPS == 0
    cut = Mesh(np.asarray(mesh.devices).reshape(ctx // 2, 2, heads_axis), ("z", "core", "head"))
    rows = P(("z", "core", "head"), None)
    return jax.shard_map(
        body,
        mesh=cut,
        in_specs=(rows,) * 8 + (P("head"),),
        out_specs=(rows, rows),
        check_vma=False,
    )
```
